32 devices in a mesh: crow: 2 (over y), ccol: 8 (over z, x), half: 2 (over core).
Axes of the slice: x: 2, y: 2, z: 4, core: 2. Of those that a mesh axis runs over, the one named last changes fastest.
Arguments:
- operator: bfloat16 [2, 8, 2048, 2048], P('crow', 'ccol', 'half'), may hold values from -0.09375 to 0.09375
- east_sources: bfloat16 [2, 8, 384, 2048], P('crow', 'ccol', None, 'half'), may hold values from -6 to 6
- west_sources: bfloat16 [2, 8, 384, 2048], P('crow', 'ccol', None, 'half'), may hold values from -6 to 6
Outputs:
- east_traces: bfloat16 [2, 8, 384, 2048], P('crow', 'ccol', None, 'half')
- west_traces: bfloat16 [2, 8, 384, 2048], P('crow', 'ccol', None, 'half')
The draws below stay inside these ranges and needn't reach their ends.
All inputs are finite; a program needn't handle non-finite values.
Results may differ from the reference program's by a relative error of at most 0.025.
Values may be sent and summed in bfloat16 or wider, within the bound.
A program may use at most 64 MiB of HBM per device.

```python
import jax
import jax.numpy as jnp
from jax import lax

TRACE = 2048
BATCH = 384
CELL_ROWS = 2
CELL_COLS = 8


def shard_levels(stream_key, dims, shards, least, top_value):
    gain, own = 1.0, jax.random.fold_in(stream_key, 6)
    for dim, blocks in shards:
        draws = jnp.exp(jax.random.uniform(jax.random.fold_in(own, dim), (blocks,), jnp.float32, least / len(shards), top_value / len(shards)))
        gain = gain * jnp.repeat(draws, dims[dim] // blocks).reshape([-1 if axis == dim else 1 for axis in range(len(dims))])
    return gain


def centred(stream_key, shape, deviation, bound, shards=(), kind=jnp.bfloat16):
    factor_of = shard_levels(stream_key, shape, shards, -0.22, 0.18) if shards else 1.0
    drawn = jax.random.normal(stream_key, shape, jnp.float32) * deviation * factor_of
    return jnp.minimum(jnp.maximum(drawn, -bound), bound).astype(kind)


def setup_inputs(seed: int = 0) -> dict:
    key_of = jax.random.split(jax.random.key(seed), 4)
    return {
        "operator": centred(key_of[0], (CELL_ROWS, CELL_COLS, TRACE, TRACE), (2 * TRACE) ** -0.5, 0.09375, ((0, 2), (1, 8), (2, 2))),
        "east_sources": centred(key_of[1], (CELL_ROWS, CELL_COLS, BATCH, TRACE), 1.0, 6.0, ((0, 2), (1, 8), (3, 2))),
        "west_sources": centred(key_of[2], (CELL_ROWS, CELL_COLS, BATCH, TRACE), 1.0, 6.0, ((0, 2), (1, 8), (3, 2))),
    }


def sweep_one(operator, sources, transpose):
    cols_total = operator.shape[1]
    batch_rows = sources.shape[2]
    trace_width = sources.shape[3]

    def row_step(upper_row, row_inputs):
        op_row, source_row = row_inputs

        def cell_step(western, inputs):
            matrix, source, from_north = inputs
            inflow = (from_north.astype(jnp.float32) + western.astype(jnp.float32)).astype(jnp.bfloat16)
            inflow = lax.optimization_barrier(inflow).astype(jnp.float32)
            dense = matrix.astype(jnp.float32)
            if transpose:
                dense = dense.T
            product = jnp.dot(inflow, dense, precision=lax.Precision.HIGHEST)
            newest = (product + source.astype(jnp.float32)).astype(jnp.bfloat16)
            return newest, newest

        start_west = jnp.zeros((batch_rows, trace_width), jnp.bfloat16)
        _, row_out = lax.scan(cell_step, start_west, (op_row, source_row, upper_row))
        return row_out, row_out

    start_row = jnp.zeros((cols_total, batch_rows, trace_width), jnp.bfloat16)
    _, traces = lax.scan(row_step, start_row, (operator, sources))
    return traces


def reference(operator, east_sources, west_sources):
    east_traces = sweep_one(operator, east_sources, True)
    flipped_op = jnp.flip(operator, axis=(0, 1))
    flipped_src = jnp.flip(west_sources, axis=(0, 1))
    west_traces = jnp.flip(sweep_one(flipped_op, flipped_src, False), axis=(0, 1))
    return east_traces, west_traces
```

```python
import functools

import jax
import jax.numpy as jnp
from jax import lax
from jax.experimental import pallas as pl
from jax.experimental.pallas import tpu as pltpu
from jax.sharding import PartitionSpec as P

BLOCKS = 12
PIECES = 4
CHUNK = 256
TILE = 256
DIRECT = 1
RELAY_AT = 9
MESH = pl.DeviceIdType.MESH


def sweeps(rows, cols, op_ref, es_ref, ws_ref, eo_ref, wo_ref,
           mats, src, from_row, from_col, relay, out, acc,
           op_sem, src_sem, row_sem, col_sem, relay_sem, out_sem, send_sem, keep_sem):
    row, col, half = lax.axis_index("crow"), lax.axis_index("ccol"), lax.axis_index("half")
    blocks, block_rows, width = es_ref.shape
    pieces, piece = from_col.shape[1], from_col.shape[3]
    mine = pieces // 2
    chunks, chunk, full = mats.shape[1:]
    own_chunks = chunks // 2
    per_piece = piece // chunk

    fwd = half == 0
    step = 1 - 2 * half
    last = cols - 1
    e_level = row + col
    w_level = rows - 1 - row + last - col
    level = jnp.where(fwd, e_level, w_level)
    e_first, w_first = e_level == 0, w_level == 0
    has_n, has_s, has_w, has_e = row > 0, row < rows - 1, col > 0, col < last
    up_row, dn_row = (fwd & has_n) | (~fwd & has_s), (fwd & has_s) | (~fwd & has_n)
    up_col, dn_col = (fwd & has_w) | (~fwd & has_e), (fwd & has_e) | (~fwd & has_w)
    next_row, next_col = {"crow": row + step}, {"ccol": col + step}
    other = {"half": 1 - half}

    mid = cols // 2
    detour = mid >= 2 and DIRECT < blocks
    src_col = mid - 1 + half
    via_col = half * last
    dst_col = mid - half
    is_src, is_via, is_dst = col == src_col, col == via_col, col == dst_col

    def local(a, b, sem):
        return pltpu.make_async_copy(a, b, sem)

    def remote(a, b, send, recv, who):
        return pltpu.make_async_remote_copy(
            src_ref=a, dst_ref=b, send_sem=send, recv_sem=recv, device_id=who, device_id_type=MESH)

    barrier = pltpu.get_barrier_semaphore()

    def greet(who):
        pl.semaphore_signal(barrier, inc=1, device_id=who, device_id_type=MESH)

    greet(other)
    for there, who in ((has_n, {"crow": row - 1}), (has_s, {"crow": row + 1}),
                       (has_w, {"ccol": col - 1}), (has_e, {"ccol": col + 1})):
        @pl.when(there)
        def _():
            for h in range(2):
                greet({**who, "half": h})
    count = 1 + 2 * (has_n.astype(jnp.int32) + has_s.astype(jnp.int32)
                     + has_w.astype(jnp.int32) + has_e.astype(jnp.int32))
    if detour:
        for there, whos in ((is_src, (via_col,)), (is_via, (src_col, dst_col)), (is_dst, (via_col,))):
            @pl.when(there)
            def _():
                for who in whos:
                    greet({"ccol": who})
        count += is_src.astype(jnp.int32) + 2 * is_via.astype(jnp.int32) + is_dst.astype(jnp.int32)

    def op_own(c):
        return local(op_ref.at[pl.ds(c * chunk, chunk)], mats.at[0, half * own_chunks + c],
                     op_sem.at[half * own_chunks + c])

    def op_give(c):
        return remote(op_ref.at[pl.ds(c * chunk, chunk)], mats.at[0, half * own_chunks + c],
                      send_sem.at[0], op_sem.at[half * own_chunks + c], other)

    def op_wait(c):
        local(op_ref.at[pl.ds(0, chunk)], mats.at[0, c], op_sem.at[c]).wait()

    def src_own(ref, q):
        p = half * mine + q
        return local(ref.at[:, :, q * piece:(q + 1) * piece], src.at[p], src_sem.at[p])

    def src_give(ref, q):
        p = half * mine + q
        return remote(ref.at[:, :, q * piece:(q + 1) * piece], src.at[p], send_sem.at[1], src_sem.at[p], other)

    def first_to(ref, k, q, buffer, sem, send, who):
        p = half * mine + q
        return remote(ref.at[k, :, q * piece:(q + 1) * piece], buffer.at[k, p], send_sem.at[send], sem.at[k, p], who)

    def firsts(ref, k, shift, h):
        return [copy for q in range(mine) for copy in (
            first_to(ref, k, q, from_col, col_sem, 2, {"ccol": col + shift, "half": h}),
            first_to(ref, k, q, from_row, row_sem, 3, {"crow": row + shift, "half": h}))]

    @pl.when(~(e_first | w_first))
    def _():
        for c in range(own_chunks):
            op_own(c).start()
    pl.semaphore_wait(barrier, count)

    for there, ref, trace, shift, h in ((e_first, es_ref, eo_ref, 1, 0), (w_first, ws_ref, wo_ref, -1, 1)):
        @pl.when(there)
        def _():
            @pl.loop(0, blocks)
            def _(k):
                for copy in firsts(ref, k, shift, h):
                    copy.start()
            local(ref, trace, keep_sem.at[h]).start()

    for c in range(own_chunks):
        op_give(c).start()

    @pl.when(e_first | w_first)
    def _():
        for c in range(own_chunks):
            op_own(c).start()

    @pl.when(fwd)
    def _():
        for q in range(mine):
            src_own(es_ref, q).start()
            src_give(ws_ref, q).start()

    @pl.when(~fwd)
    def _():
        for q in range(mine):
            src_own(ws_ref, q).start()
            src_give(es_ref, q).start()

    for there, buffer in ((up_row, from_row), (up_col, from_col)):
        @pl.when(~there)
        def _():
            @pl.loop(0, blocks)
            def _(k):
                buffer[k] = jnp.zeros(buffer.shape[1:], buffer.dtype)

    @pl.loop(0, chunks)
    def _(c):
        op_wait(c)

        @pl.when(fwd & (level > 0))
        def _():
            at = pl.multiple_of(c * chunk, chunk)
            for n in range(chunks):
                mats[1, n, :, pl.ds(at, chunk)] = mats[0, c, :, n * chunk:(n + 1) * chunk].T
    for p in range(pieces):
        local(es_ref.at[:, :, :piece], src.at[p], src_sem.at[p]).wait()

    use = 1 - half

    def to_row(k, p):
        return remote(out.at[k, p], from_row.at[k, p], send_sem.at[3], row_sem.at[k, p], next_row)

    def to_col(k, p):
        return remote(out.at[k, p], from_col.at[k, p], send_sem.at[2], col_sem.at[k, p], next_col)

    def to_via(k, p):
        return remote(out.at[k, p], relay.at[k, p], send_sem.at[2], relay_sem.at[k, p], {"ccol": via_col})

    def from_via(k, p):
        return remote(relay.at[k, p], from_col.at[k, p], send_sem.at[4], col_sem.at[k, p], {"ccol": dst_col})

    def keep(trace, k, p):
        return local(out.at[k, p], trace.at[k, :, (p % mine) * piece:(p % mine + 1) * piece], keep_sem.at[half])

    def give(trace, k, p):
        return remote(out.at[k, p], trace.at[k, :, (p % mine) * piece:(p % mine + 1) * piece],
                      send_sem.at[5], out_sem.at[0], other)

    def send(k, p):
        far = is_src & (k >= DIRECT)
        if detour:
            @pl.when(far)
            def _():
                to_via(k, p).start()

            @pl.when(dn_col & ~far)
            def _():
                to_col(k, p).start()
        else:
            @pl.when(dn_col)
            def _():
                to_col(k, p).start()

        @pl.when(dn_row)
        def _():
            to_row(k, p).start()

        @pl.when(fwd)
        def _():
            (keep if p < mine else give)(eo_ref, k, p).start()

        @pl.when(~fwd)
        def _():
            (give if p < mine else keep)(wo_ref, k, p).start()

    @pl.loop(0, blocks + (RELAY_AT if detour else 0))
    def _(s):
        if detour:
            j = s - RELAY_AT

            @pl.when(is_via & (j >= DIRECT))
            def _():
                for p in range(pieces):
                    to_via(j, p).wait_recv()
                    from_via(j, p).start()

        @pl.when((level > 0) & (s < blocks))
        def _():
            for p in range(pieces):
                @pl.when(up_row)
                def _():
                    to_row(s, p).wait_recv()

                @pl.when(up_col)
                def _():
                    to_col(s, p).wait_recv()
                x = (from_row[s, p].astype(jnp.float32) + from_col[s, p].astype(jnp.float32)).astype(jnp.bfloat16)
                for n in range(0, full, TILE):
                    weights = mats[use, p * per_piece:(p + 1) * per_piece, :, n:n + TILE].reshape(piece, TILE)
                    part = jnp.dot(x, weights, preferred_element_type=jnp.float32)
                    o, at = n // piece, n % piece
                    if p == 0:
                        acc[:, n:n + TILE] = part + src[o, s, :, at:at + TILE].astype(jnp.float32)
                    elif p < pieces - 1:
                        acc[:, n:n + TILE] += part
                    else:
                        out[s, o, :, at:at + TILE] = (acc[:, n:n + TILE] + part).astype(jnp.bfloat16)
                        if n + TILE in (piece, full):
                            for ready in range(0 if n < piece else 1, o + 1):
                                send(s, ready)

    for c in range(own_chunks):
        op_give(c).wait_send()
    for q in range(mine):
        src_give(es_ref, q).wait_send()
    for there, ref, trace, shift, h in ((e_first, es_ref, eo_ref, 1, 0), (w_first, ws_ref, wo_ref, -1, 1)):
        @pl.when(there)
        def _():
            @pl.loop(0, blocks)
            def _(k):
                for copy in firsts(ref, k, shift, h):
                    copy.wait_send()
            local(ref, trace, keep_sem.at[h]).wait()

    @pl.when(level > 0)
    def _():
        @pl.when(dn_row)
        def _():
            remote(out, from_row, send_sem.at[3], row_sem.at[0, 0], next_row).wait_send()

        @pl.when(dn_col)
        def _():
            remote(out, from_col, send_sem.at[2], col_sem.at[0, 0], next_col).wait_send()
        local(eo_ref, eo_ref, keep_sem.at[half]).wait()
        remote(eo_ref, eo_ref, send_sem.at[5], out_sem.at[0], other).wait_send()
    if detour:
        @pl.when(is_via)
        def _():
            some = pl.ds(DIRECT, blocks - DIRECT)
            remote(relay.at[some], from_col.at[some], send_sem.at[4], col_sem.at[0, 0], {"ccol": dst_col}).wait_send()

    @pl.when((fwd & ~w_first) | (~fwd & ~e_first))
    def _():
        remote(eo_ref, eo_ref, send_sem.at[5], out_sem.at[0], other).wait_recv()


def local(rows, cols, operator, east_sources, west_sources):
    matrix = operator[0, 0]
    batch, width = east_sources.shape[2:]
    blocks, block_rows = BLOCKS, batch // BLOCKS
    cut = (blocks, block_rows, width)
    full = 2 * width
    piece = full // PIECES
    trace = pltpu.VMEM((blocks, PIECES, block_rows, piece), jnp.bfloat16)
    dma = pltpu.SemaphoreType.DMA
    hbm = functools.partial(pltpu.with_memory_space_constraint, memory_space=pltpu.HBM)
    east, west = pl.pallas_call(
        functools.partial(sweeps, rows, cols),
        out_shape=[jax.ShapeDtypeStruct(cut, jnp.bfloat16)] * 2,
        in_specs=[pl.BlockSpec(memory_space=pltpu.HBM)] * 3,
        out_specs=[pl.BlockSpec(memory_space=pltpu.VMEM)] * 2,
        scratch_shapes=[
            pltpu.VMEM((2, full // CHUNK, CHUNK, full), jnp.bfloat16),
            pltpu.VMEM((PIECES, blocks, block_rows, piece), jnp.bfloat16),
            trace, trace, trace, trace,
            pltpu.VMEM((block_rows, full), jnp.float32),
            dma((full // CHUNK,)), dma((PIECES,)),
            dma((blocks, PIECES)), dma((blocks, PIECES)), dma((blocks, PIECES)),
            dma((1,)), dma((6,)), dma((2,)),
        ],
        compiler_params=pltpu.CompilerParams(
            collective_id=0, has_side_effects=True, vmem_limit_bytes=32 * 2**20),
        name="sweeps",
    )(hbm(matrix), hbm(east_sources.reshape(cut)), hbm(west_sources.reshape(cut)))
    return east.reshape(1, 1, batch, width), west.reshape(1, 1, batch, width)


def solution(mesh):
    in_specs = (
        P("crow", "ccol", "half", None),
        P("crow", "ccol", None, "half"),
        P("crow", "ccol", None, "half"),
    )
    out_specs = (P("crow", "ccol", None, "half"), P("crow", "ccol", None, "half"))
    body = functools.partial(local, mesh.shape["crow"], mesh.shape["ccol"])
    return jax.shard_map(body, mesh=mesh, in_specs=in_specs, out_specs=out_specs, check_vma=False)
```

```python
import functools

import jax
import jax.numpy as jnp
from jax import lax
from jax.experimental import pallas as pl
from jax.experimental.pallas import tpu as pltpu
from jax.sharding import PartitionSpec as P

BLOCKS = 12
PIECES = 4
CHUNK = 256
TILE = 256
NEAR_LEAD, NEAR_REST = ((12, 12, 4), (12, 12, 4), (12, 12, 4)), ((8, 12, 4), (12, 12, 4), (12, 12, 4))
LONG_LEAD, LONG_REST = (0, 9), (1, 6)
NEAR_OFF, BACK_OFF, AHEAD_OFF = 4, 8, -7
MESH = pl.DeviceIdType.MESH


def sweeps(rows, cols, op_ref, es_ref, ws_ref, eo_ref, wo_ref,
           mats, src, from_row, inbox, out, acc, zeros,
           op_sem, src_sem, row_sem, col_sem, out_sem, send_sem, keep_sem):
    row, col, half = lax.axis_index("crow"), lax.axis_index("ccol"), lax.axis_index("half")
    blocks, block_rows, width = es_ref.shape
    pieces, piece = from_row.shape[1], from_row.shape[3]
    mine = pieces // 2
    chunks, chunk, full = mats.shape[1:]
    own_chunks = chunks // 2
    per_piece = piece // chunk

    fwd = half == 0
    step = 1 - 2 * half
    last = cols - 1
    e_level = row + col
    w_level = rows - 1 - row + last - col
    level = jnp.where(fwd, e_level, w_level)
    e_first, w_first = e_level == 0, w_level == 0
    has_n, has_s, has_w, has_e = row > 0, row < rows - 1, col > 0, col < last
    up_row, dn_row = (fwd & has_n) | (~fwd & has_s), (fwd & has_s) | (~fwd & has_n)
    up_col, dn_col = (fwd & has_w) | (~fwd & has_e), (fwd & has_e) | (~fwd & has_w)
    next_row, next_col = {"crow": row + step}, {"ccol": col + step}
    other = {"half": 1 - half}

    place = jnp.where(fwd, col, last - col)
    lead = jnp.where(fwd, row == 0, row == rows - 1)
    turns = (cols - 1) // 2
    detour = turns > 0
    middle = 2 * (turns // 2) + 1
    odd = place % 2 == 1
    def pick(cases, default):
        for cond, value in cases:
            default = jnp.where(cond, value, default)
        return default

    def at(where_to):
        return {"ccol": jnp.where(fwd, where_to, last - where_to)}

    def near_of(turn):
        kind = pick(((turn < turns // 2, 0), (turn == turns // 2, 1)), 2)
        values = [pick([(lead & (kind == i), NEAR_LEAD[i][v]) for i in range(3)]
                       + [(~lead & (kind == i), NEAR_REST[i][v]) for i in range(3)], 0) for v in range(3)]
        return jnp.minimum(values[0], blocks), jnp.minimum(values[1], blocks), values[2]

    def long_of():
        first, end = (pick(((lead, LONG_LEAD[v]),), LONG_REST[v]) for v in range(2))
        return jnp.minimum(first, blocks), jnp.minimum(end, blocks)

    can_near = odd & (place < last)
    can_long = (place == middle) & (lead | (middle + 3 <= last))
    near_first, near_end, near_pieces = near_of(place // 2)
    long_first, long_end = long_of()
    long_place = jnp.where(lead, 0, middle + 3)
    is_near = ~odd & (place + 2 <= last)
    is_long = (place == long_place) & (middle + 1 <= last)
    to_near = ~odd & (place >= 2)
    to_long = (place == middle + 1) & (long_place <= last)

    def local(a, b, sem):
        return pltpu.make_async_copy(a, b, sem)

    def remote(a, b, send, recv, who):
        return pltpu.make_async_remote_copy(
            src_ref=a, dst_ref=b, send_sem=send, recv_sem=recv, device_id=who, device_id_type=MESH)

    zeros[...] = jnp.zeros_like(zeros)
    barrier = pltpu.get_barrier_semaphore()

    def greet(who):
        pl.semaphore_signal(barrier, inc=1, device_id=who, device_id_type=MESH)

    greet(other)
    for there, who in ((has_n, {"crow": row - 1}), (has_s, {"crow": row + 1}),
                       (has_w, {"ccol": col - 1}), (has_e, {"ccol": col + 1})):
        @pl.when(there)
        def _():
            for h in range(2):
                greet({**who, "half": h})
    count = 1 + 2 * (has_n.astype(jnp.int32) + has_s.astype(jnp.int32)
                     + has_w.astype(jnp.int32) + has_e.astype(jnp.int32))
    if detour:
        for there, whos in ((can_near, (place - 1,)), (is_near, (place + 1, place + 2)), (to_near, (place - 2,)),
                            (can_long, (long_place,)), (is_long, (middle, middle + 1)), (to_long, (long_place,))):
            @pl.when(there)
            def _():
                for who in whos:
                    greet(at(who))
            count += len(whos) * there.astype(jnp.int32)

    def op_own(c):
        return local(op_ref.at[pl.ds(c * chunk, chunk)], mats.at[0, half * own_chunks + c],
                     op_sem.at[half * own_chunks + c])

    def op_give(c):
        return remote(op_ref.at[pl.ds(c * chunk, chunk)], mats.at[0, half * own_chunks + c],
                      send_sem.at[0], op_sem.at[half * own_chunks + c], other)

    def op_wait(c):
        local(op_ref.at[pl.ds(0, chunk)], mats.at[0, c], op_sem.at[c]).wait()

    def src_own(ref, q):
        p = half * mine + q
        return local(ref.at[:, :, q * piece:(q + 1) * piece], src.at[p], src_sem.at[p])

    def src_give(ref, q):
        p = half * mine + q
        return remote(ref.at[:, :, q * piece:(q + 1) * piece], src.at[p], send_sem.at[1], src_sem.at[p], other)

    def first_to(ref, k, q, buffer, sem, send, who):
        p = half * mine + q
        return remote(ref.at[k, :, q * piece:(q + 1) * piece], buffer.at[k, p], send_sem.at[send], sem.at[k, p], who)

    def firsts(ref, k, shift, h):
        return [copy for q in range(mine) for copy in (
            first_to(ref, k, q, inbox.at[0], col_sem.at[0], 2, {"ccol": col + shift, "half": h}),
            first_to(ref, k, q, from_row, row_sem, 3, {"crow": row + shift, "half": h}))]

    @pl.when(~(e_first | w_first))
    def _():
        for c in range(own_chunks):
            op_own(c).start()
    pl.semaphore_wait(barrier, count)

    for there, ref, trace, shift, h in ((e_first, es_ref, eo_ref, 1, 0), (w_first, ws_ref, wo_ref, -1, 1)):
        @pl.when(there)
        def _():
            @pl.loop(0, blocks)
            def _(k):
                for copy in firsts(ref, k, shift, h):
                    copy.start()
            local(ref, trace, keep_sem.at[h]).start()

    for c in range(own_chunks):
        op_give(c).start()

    @pl.when(e_first | w_first)
    def _():
        for c in range(own_chunks):
            op_own(c).start()

    @pl.when(fwd)
    def _():
        for q in range(mine):
            src_own(es_ref, q).start()
            src_give(ws_ref, q).start()

    @pl.when(~fwd)
    def _():
        for q in range(mine):
            src_own(ws_ref, q).start()
            src_give(es_ref, q).start()

    share = pl.cdiv(blocks, chunks)

    @pl.loop(0, chunks)
    def _(c):
        for there, buffer, sem in ((up_row, from_row, row_sem), (up_col, inbox.at[0], col_sem.at[0])):
            @pl.when((level > 0) & ~there)
            def _():
                @pl.loop(jnp.minimum(c * share, blocks), jnp.minimum(c * share + share, blocks))
                def _(k):
                    for p in range(pieces):
                        local(zeros, buffer.at[k, p], sem.at[k, p]).start()
        op_wait(c)

        @pl.when(fwd & (level > 0))
        def _():
            at = pl.multiple_of(c * chunk, chunk)
            for n in range(chunks):
                mats[1, n, :, pl.ds(at, chunk)] = mats[0, c, :, n * chunk:(n + 1) * chunk].T
    for p in range(pieces):
        local(es_ref.at[:, :, :piece], src.at[p], src_sem.at[p]).wait()

    use = 1 - half

    def to_row(k, p):
        return remote(out.at[k, p], from_row.at[k, p], send_sem.at[3], row_sem.at[k, p], next_row)

    def to_col(k, p):
        by_near = can_near & (k >= near_first) & (k < near_end) & (p < near_pieces)
        by_long = can_long & (k >= long_first) & (k < long_end)
        box = pick(((by_long, 2), (by_near, 1)), 0)
        who = at(pick(((by_long, long_place), (by_near, place - 1)), place + 1))
        return remote(out.at[k, p], inbox.at[box, k, p], send_sem.at[2], col_sem.at[box, k, p], who)

    def col_in(k, p):
        return local(zeros, inbox.at[0, k, p], col_sem.at[0, k, p])

    def row_in(k, p):
        return local(zeros, from_row.at[k, p], row_sem.at[k, p])

    def via_in(box, k, p):
        return local(zeros, inbox.at[box, k, p], col_sem.at[box, k, p])

    def pass_on(box, k, p):
        return remote(inbox.at[box, k, p], inbox.at[0, k, p], send_sem.at[4], col_sem.at[0, k, p],
                      at(place + 2 if box == 1 else middle + 1))

    def keep(trace, k, p):
        return local(out.at[k, p], trace.at[k, :, (p % mine) * piece:(p % mine + 1) * piece], keep_sem.at[half])

    def give(trace, k, p):
        return remote(out.at[k, p], trace.at[k, :, (p % mine) * piece:(p % mine + 1) * piece],
                      send_sem.at[5], out_sem.at[0], other)

    def send(k, some):
        @pl.when(dn_col)
        def _():
            for p in some:
                to_col(k, p).start()

        @pl.when(dn_row)
        def _():
            for p in some:
                to_row(k, p).start()

    def own(s, p):
        row_in(s, p).wait()
        col_in(s, p).wait()
        x = (from_row[s, p].astype(jnp.float32) + inbox[0, s, p].astype(jnp.float32)).astype(jnp.bfloat16)
        for n in range(0, full, TILE):
            weights = mats[use, p * per_piece:(p + 1) * per_piece, :, n:n + TILE].reshape(piece, TILE)
            part = jnp.dot(x, weights, preferred_element_type=jnp.float32)
            o, at = n // piece, n % piece
            if p == 0:
                acc[:, n:n + TILE] = part + src[o, s, :, at:at + TILE].astype(jnp.float32)
            elif p < pieces - 1:
                acc[:, n:n + TILE] += part
            else:
                out[s, o, :, at:at + TILE] = (acc[:, n:n + TILE] + part).astype(jnp.bfloat16)
                if n + TILE == piece:
                    send(s, (0,))
                if n + TILE == full:
                    send(s, range(1, pieces))

    def store(s):
        @pl.when(fwd)
        def _():
            for p in range(pieces):
                (keep if p < mine else give)(eo_ref, s, p).start()

        @pl.when(~fwd)
        def _():
            for p in range(pieces):
                (give if p < mine else keep)(wo_ref, s, p).start()

    hop_first, hop_end, hop_pieces = near_of(place // 2)
    long_off = jnp.where(lead, BACK_OFF, AHEAD_OFF)
    is_via = is_near & (hop_end > hop_first) | is_long & (long_end > long_first)

    def relay(t):
        @pl.when(is_via)
        def _():
            k = t - NEAR_OFF

            @pl.when(is_near & (k >= hop_first) & (k < hop_end))
            def _():
                @pl.loop(0, hop_pieces)
                def _(p):
                    via_in(1, k, p).wait()
                    pass_on(1, k, p).start()
            m = t - long_off

            @pl.when(is_long & (m >= long_first) & (m < long_end))
            def _():
                for p in range(pieces):
                    via_in(2, m, p).wait()
                    pass_on(2, m, p).start()

    if detour:
        @pl.loop(min(AHEAD_OFF, 0), 0)
        def _(t):
            relay(t)

    @pl.when(level > 0)
    def _():
        @pl.loop(0, blocks)
        def _(s):
            for p in range(pieces):
                own(s, p)
            store(s)
            if detour:
                relay(s)

    if detour:
        @pl.loop(jnp.where(level > 0, blocks, 0), blocks + max(NEAR_OFF, BACK_OFF))
        def _(t):
            relay(t)

    for c in range(own_chunks):
        op_give(c).wait_send()
    for q in range(mine):
        src_give(es_ref, q).wait_send()
    for there, ref, trace, shift, h in ((e_first, es_ref, eo_ref, 1, 0), (w_first, ws_ref, wo_ref, -1, 1)):
        @pl.when(there)
        def _():
            @pl.loop(0, blocks)
            def _(k):
                for copy in firsts(ref, k, shift, h):
                    copy.wait_send()
            local(ref, trace, keep_sem.at[h]).wait()

    @pl.when(level > 0)
    def _():
        @pl.when(dn_row)
        def _():
            remote(out, from_row, send_sem.at[3], row_sem.at[0, 0], next_row).wait_send()

        @pl.when(dn_col)
        def _():
            remote(out, from_row, send_sem.at[2], row_sem.at[0, 0], next_col).wait_send()
        local(eo_ref, eo_ref, keep_sem.at[half]).wait()
        remote(eo_ref, eo_ref, send_sem.at[5], out_sem.at[0], other).wait_send()
    if detour:
        for there, box, first, end, some in ((is_near, 1, hop_first, hop_end, hop_pieces),
                                             (is_long, 2, long_first, long_end, pieces)):
            @pl.when(there)
            def _():
                @pl.loop(first, end)
                def _(k):
                    @pl.loop(0, some)
                    def _(p):
                        pass_on(box, k, p).wait_send()

    @pl.when((fwd & ~w_first) | (~fwd & ~e_first))
    def _():
        remote(eo_ref, eo_ref, send_sem.at[5], out_sem.at[0], other).wait_recv()


def flush(east, west, east_out, west_out, sem):
    copies = [pltpu.make_async_copy(a, b, sem.at[i])
              for i, (a, b) in enumerate(((east, east_out), (west, west_out)))]
    for copy in copies:
        copy.start()
    for copy in copies:
        copy.wait()


def local(rows, cols, operator, east_sources, west_sources):
    matrix = operator[0, 0]
    batch, width = east_sources.shape[2:]
    blocks, block_rows = BLOCKS, batch // BLOCKS
    cut = (blocks, block_rows, width)
    full = 2 * width
    piece = full // PIECES
    cells = (blocks, PIECES, block_rows, piece)
    trace = pltpu.VMEM(cells, jnp.bfloat16)
    dma = pltpu.SemaphoreType.DMA
    hbm = functools.partial(pltpu.with_memory_space_constraint, memory_space=pltpu.HBM)
    east, west = pl.pallas_call(
        functools.partial(sweeps, rows, cols),
        out_shape=[jax.ShapeDtypeStruct(cut, jnp.bfloat16)] * 2,
        in_specs=[pl.BlockSpec(memory_space=pltpu.HBM)] * 3,
        out_specs=[pl.BlockSpec(memory_space=pltpu.VMEM)] * 2,
        scratch_shapes=[
            pltpu.VMEM((2, full // CHUNK, CHUNK, full), jnp.bfloat16),
            pltpu.VMEM((PIECES, blocks, block_rows, piece), jnp.bfloat16),
            trace,
            pltpu.VMEM((3, *cells), jnp.bfloat16),
            trace,
            pltpu.VMEM((block_rows, full), jnp.float32),
            pltpu.VMEM((block_rows, piece), jnp.bfloat16),
            dma((full // CHUNK,)), dma((PIECES,)),
            dma((blocks, PIECES)), dma((3, blocks, PIECES)),
            dma((1,)), dma((6,)), dma((2,)),
        ],
        compiler_params=pltpu.CompilerParams(
            collective_id=0, has_side_effects=True, vmem_limit_bytes=32 * 2**20),
        name="sweeps",
    )(hbm(matrix), hbm(east_sources.reshape(cut)), hbm(west_sources.reshape(cut)))
    anywhere = pl.BlockSpec(memory_space=pl.ANY)
    east, west = pl.pallas_call(
        flush,
        out_shape=[jax.ShapeDtypeStruct(cut, jnp.bfloat16)] * 2,
        in_specs=[anywhere] * 2,
        out_specs=[anywhere] * 2,
        scratch_shapes=[dma((2,))],
        compiler_params=pltpu.CompilerParams(vmem_limit_bytes=2**20),
        name="flush",
    )(east, west)
    return east.reshape(1, 1, batch, width), west.reshape(1, 1, batch, width)


def solution(mesh):
    in_specs = (
        P("crow", "ccol", "half", None),
        P("crow", "ccol", None, "half"),
        P("crow", "ccol", None, "half"),
    )
    out_specs = (P("crow", "ccol", None, "half"), P("crow", "ccol", None, "half"))
    body = functools.partial(local, mesh.shape["crow"], mesh.shape["ccol"])
    return jax.shard_map(body, mesh=mesh, in_specs=in_specs, out_specs=out_specs, check_vma=False)
```

```python
import functools

import jax
import jax.numpy as jnp
from jax import lax
from jax.experimental import pallas as pl
from jax.experimental.pallas import tpu as pltpu
from jax.sharding import PartitionSpec as P

BLOCKS = 12
PIECES = 4
CHUNK = 256
TILE = 256
NEAR_LEAD, NEAR_REST = ((12, 12, 4), (12, 12, 4), (12, 12, 4)), ((8, 12, 4), (12, 12, 4), (12, 12, 4))
LONG_LEAD, LONG_REST = (0, 9), (1, 6)
NEAR_OFF, BACK_OFF, AHEAD_OFF = 4, 8, -7
MESH = pl.DeviceIdType.MESH


def sweeps(rows, cols, op_ref, es_ref, ws_ref, eo_ref, wo_ref,
           mats, src, from_row, inbox, out, acc, zeros,
           op_sem, src_sem, row_sem, col_sem, out_sem, send_sem, keep_sem):
    row, col, half = lax.axis_index("crow"), lax.axis_index("ccol"), lax.axis_index("half")
    blocks, block_rows, width = es_ref.shape
    pieces, piece = from_row.shape[1], from_row.shape[3]
    mine = pieces // 2
    chunks, chunk, full = mats.shape[1:]
    own_chunks = chunks // 2
    per_piece = piece // chunk

    fwd = half == 0
    step = 1 - 2 * half
    last = cols - 1
    e_level = row + col
    w_level = rows - 1 - row + last - col
    level = jnp.where(fwd, e_level, w_level)
    e_first, w_first = e_level == 0, w_level == 0
    has_n, has_s, has_w, has_e = row > 0, row < rows - 1, col > 0, col < last
    up_row, dn_row = (fwd & has_n) | (~fwd & has_s), (fwd & has_s) | (~fwd & has_n)
    up_col, dn_col = (fwd & has_w) | (~fwd & has_e), (fwd & has_e) | (~fwd & has_w)
    next_row, next_col = {"crow": row + step}, {"ccol": col + step}
    other = {"half": 1 - half}

    place = jnp.where(fwd, col, last - col)
    lead = jnp.where(fwd, row == 0, row == rows - 1)
    turns = (cols - 1) // 2
    detour = turns > 0
    middle = 2 * (turns // 2) + 1
    odd = place % 2 == 1
    def pick(cases, default):
        for cond, value in cases:
            default = jnp.where(cond, value, default)
        return default

    def at(where_to):
        return {"ccol": jnp.where(fwd, where_to, last - where_to)}

    def near_of(turn):
        kind = pick(((turn < turns // 2, 0), (turn == turns // 2, 1)), 2)
        values = [pick([(lead & (kind == i), NEAR_LEAD[i][v]) for i in range(3)]
                       + [(~lead & (kind == i), NEAR_REST[i][v]) for i in range(3)], 0) for v in range(3)]
        return jnp.minimum(values[0], blocks), jnp.minimum(values[1], blocks), values[2]

    def long_of():
        first, end = (pick(((lead, LONG_LEAD[v]),), LONG_REST[v]) for v in range(2))
        return jnp.minimum(first, blocks), jnp.minimum(end, blocks)

    can_near = odd & (place < last)
    can_long = (place == middle) & (lead | (middle + 3 <= last))
    near_first, near_end, near_pieces = near_of(place // 2)
    long_first, long_end = long_of()
    long_place = jnp.where(lead, 0, middle + 3)
    is_near = ~odd & (place + 2 <= last)
    is_long = (place == long_place) & (middle + 1 <= last)
    to_near = ~odd & (place >= 2)
    to_long = (place == middle + 1) & (long_place <= last)

    def local(a, b, sem):
        return pltpu.make_async_copy(a, b, sem)

    def remote(a, b, send, recv, who):
        return pltpu.make_async_remote_copy(
            src_ref=a, dst_ref=b, send_sem=send, recv_sem=recv, device_id=who, device_id_type=MESH)

    zeros[...] = jnp.zeros_like(zeros)
    barrier = pltpu.get_barrier_semaphore()

    def greet(who):
        pl.semaphore_signal(barrier, inc=1, device_id=who, device_id_type=MESH)

    greet(other)
    for there, who in ((has_n, {"crow": row - 1}), (has_s, {"crow": row + 1}),
                       (has_w, {"ccol": col - 1}), (has_e, {"ccol": col + 1})):
        @pl.when(there)
        def _():
            for h in range(2):
                greet({**who, "half": h})
    count = 1 + 2 * (has_n.astype(jnp.int32) + has_s.astype(jnp.int32)
                     + has_w.astype(jnp.int32) + has_e.astype(jnp.int32))
    if detour:
        for there, whos in ((can_near, (place - 1,)), (is_near, (place + 1, place + 2)), (to_near, (place - 2,)),
                            (can_long, (long_place,)), (is_long, (middle, middle + 1)), (to_long, (long_place,))):
            @pl.when(there)
            def _():
                for who in whos:
                    greet(at(who))
            count += len(whos) * there.astype(jnp.int32)

    def op_own(c):
        return local(op_ref.at[pl.ds(c * chunk, chunk)], mats.at[0, half * own_chunks + c],
                     op_sem.at[half * own_chunks + c])

    def op_give(c):
        return remote(op_ref.at[pl.ds(c * chunk, chunk)], mats.at[0, half * own_chunks + c],
                      send_sem.at[0], op_sem.at[half * own_chunks + c], other)

    def op_wait(c):
        local(op_ref.at[pl.ds(0, chunk)], mats.at[0, c], op_sem.at[c]).wait()

    def src_own(ref, q):
        p = half * mine + q
        return local(ref.at[:, :, q * piece:(q + 1) * piece], src.at[p], src_sem.at[p])

    def src_give(ref, q):
        p = half * mine + q
        return remote(ref.at[:, :, q * piece:(q + 1) * piece], src.at[p], send_sem.at[1], src_sem.at[p], other)

    def first_to(ref, k, q, buffer, sem, send, who):
        p = half * mine + q
        return remote(ref.at[k, :, q * piece:(q + 1) * piece], buffer.at[k, p], send_sem.at[send], sem.at[k, p], who)

    def firsts(ref, k, shift, h):
        return [copy for q in range(mine) for copy in (
            first_to(ref, k, q, inbox, col_sem, 2, {"ccol": col + shift, "half": h}),
            first_to(ref, k, q, from_row, row_sem, 3, {"crow": row + shift, "half": h}))]

    @pl.when(~(e_first | w_first))
    def _():
        for c in range(own_chunks):
            op_own(c).start()
    pl.semaphore_wait(barrier, count)

    for there, ref, trace, shift, h in ((e_first, es_ref, eo_ref, 1, 0), (w_first, ws_ref, wo_ref, -1, 1)):
        @pl.when(there)
        def _():
            @pl.loop(0, blocks)
            def _(k):
                for copy in firsts(ref, k, shift, h):
                    copy.start()
            local(ref, trace, keep_sem.at[h]).start()

    for c in range(own_chunks):
        op_give(c).start()

    @pl.when(e_first | w_first)
    def _():
        for c in range(own_chunks):
            op_own(c).start()

    @pl.when(fwd)
    def _():
        for q in range(mine):
            src_own(es_ref, q).start()
            src_give(ws_ref, q).start()

    @pl.when(~fwd)
    def _():
        for q in range(mine):
            src_own(ws_ref, q).start()
            src_give(es_ref, q).start()

    share = pl.cdiv(blocks - 1, own_chunks)

    @pl.loop(0, chunks)
    def _(c):
        for there, buffer, sem in ((up_row, from_row, row_sem), (up_col, inbox, col_sem)):
            @pl.when((level > 0) & ~there)
            def _():
                begin = jnp.where(c < own_chunks, jnp.minimum(c, 1), 1 + share * (c - own_chunks))
                end = jnp.where(c < own_chunks, 1, begin + share)

                @pl.loop(jnp.minimum(begin, blocks), jnp.minimum(end, blocks))
                def _(k):
                    for p in range(pieces):
                        local(zeros, buffer.at[k, p], sem.at[k, p]).start()
        op_wait(c)

        @pl.when(fwd & (level > 0))
        def _():
            at = pl.multiple_of(c * chunk, chunk)
            for n in range(chunks):
                mats[1, n, :, pl.ds(at, chunk)] = mats[0, c, :, n * chunk:(n + 1) * chunk].T
    for p in range(pieces):
        local(es_ref.at[:, :, :piece], src.at[p], src_sem.at[p]).wait()

    use = 1 - half

    def to_row(k, p):
        return remote(out.at[k, p], from_row.at[k, p], send_sem.at[3], row_sem.at[k, p], next_row)

    def to_col(k, p):
        by_near = can_near & (k >= near_first) & (k < near_end) & (p < near_pieces)
        by_long = can_long & (k >= long_first) & (k < long_end)
        box = jnp.where(by_long | by_near, 1, 0)
        slot = k - pick(((by_long, long_first), (by_near, near_first)), 0)
        who = at(pick(((by_long, long_place), (by_near, place - 1)), place + 1))
        return remote(out.at[k, p], inbox.at[box * blocks + slot, p], send_sem.at[2], col_sem.at[box * blocks + slot, p], who)

    def col_in(k, p):
        return local(zeros, inbox.at[k, p], col_sem.at[k, p])

    def row_in(k, p):
        return local(zeros, from_row.at[k, p], row_sem.at[k, p])

    def slot_of(box, k):
        return blocks + k - (hop_first if box == 1 else long_first)

    def via_in(box, k, p):
        return local(zeros, inbox.at[slot_of(box, k), p], col_sem.at[slot_of(box, k), p])

    def pass_on(box, k, p):
        return remote(inbox.at[slot_of(box, k), p], inbox.at[k, p], send_sem.at[4], col_sem.at[k, p],
                      at(place + 2 if box == 1 else middle + 1))

    def keep(trace, k, p):
        return local(out.at[k, p], trace.at[k, :, (p % mine) * piece:(p % mine + 1) * piece], keep_sem.at[half])

    def give(trace, k, p):
        return remote(out.at[k, p], trace.at[k, :, (p % mine) * piece:(p % mine + 1) * piece],
                      send_sem.at[5], out_sem.at[0], other)

    def send(k, some):
        @pl.when(dn_col)
        def _():
            for p in some:
                to_col(k, p).start()

        @pl.when(dn_row)
        def _():
            for p in some:
                to_row(k, p).start()

    def own(s, p):
        row_in(s, p).wait()
        col_in(s, p).wait()
        x = (from_row[s, p].astype(jnp.float32) + inbox[s, p].astype(jnp.float32)).astype(jnp.bfloat16)
        for n in range(0, full, TILE):
            weights = mats[use, p * per_piece:(p + 1) * per_piece, :, n:n + TILE].reshape(piece, TILE)
            part = jnp.dot(x, weights, preferred_element_type=jnp.float32)
            o, at = n // piece, n % piece
            if p == 0:
                acc[:, n:n + TILE] = part + src[o, s, :, at:at + TILE].astype(jnp.float32)
            elif p < pieces - 1:
                acc[:, n:n + TILE] += part
            else:
                out[s, o, :, at:at + TILE] = (acc[:, n:n + TILE] + part).astype(jnp.bfloat16)
                if n + TILE == piece:
                    send(s, (0,))
                if n + TILE == full:
                    send(s, range(1, pieces))

    def store(s):
        @pl.when(fwd)
        def _():
            for p in range(pieces):
                (keep if p < mine else give)(eo_ref, s, p).start()

        @pl.when(~fwd)
        def _():
            for p in range(pieces):
                (give if p < mine else keep)(wo_ref, s, p).start()

    hop_first, hop_end, hop_pieces = near_of(place // 2)
    long_off = jnp.where(lead, BACK_OFF, AHEAD_OFF)
    is_via = is_near & (hop_end > hop_first) | is_long & (long_end > long_first)

    def relay(t):
        @pl.when(is_via)
        def _():
            k = t - NEAR_OFF

            @pl.when(is_near & (k >= hop_first) & (k < hop_end))
            def _():
                @pl.loop(0, hop_pieces)
                def _(p):
                    via_in(1, k, p).wait()
                    pass_on(1, k, p).start()
            m = t - long_off

            @pl.when(is_long & (m >= long_first) & (m < long_end))
            def _():
                for p in range(pieces):
                    via_in(2, m, p).wait()
                    pass_on(2, m, p).start()

    if detour:
        @pl.loop(min(AHEAD_OFF, 0), 0)
        def _(t):
            relay(t)

    @pl.when(level > 0)
    def _():
        @pl.loop(0, blocks)
        def _(s):
            for p in range(pieces):
                own(s, p)
            store(s)
            if detour:
                relay(s)

    if detour:
        @pl.loop(jnp.where(level > 0, blocks, 0), blocks + max(NEAR_OFF, BACK_OFF))
        def _(t):
            relay(t)

    for c in range(own_chunks):
        op_give(c).wait_send()
    for q in range(mine):
        src_give(es_ref, q).wait_send()
    for there, ref, trace, shift, h in ((e_first, es_ref, eo_ref, 1, 0), (w_first, ws_ref, wo_ref, -1, 1)):
        @pl.when(there)
        def _():
            @pl.loop(0, blocks)
            def _(k):
                for copy in firsts(ref, k, shift, h):
                    copy.wait_send()
            local(ref, trace, keep_sem.at[h]).wait()

    @pl.when(level > 0)
    def _():
        @pl.when(dn_row)
        def _():
            remote(out, from_row, send_sem.at[3], row_sem.at[0, 0], next_row).wait_send()

        @pl.when(dn_col)
        def _():
            remote(out, from_row, send_sem.at[2], row_sem.at[0, 0], next_col).wait_send()
        local(eo_ref, eo_ref, keep_sem.at[half]).wait()
        remote(eo_ref, eo_ref, send_sem.at[5], out_sem.at[0], other).wait_send()
    if detour:
        for there, box, first, end, some in ((is_near, 1, hop_first, hop_end, hop_pieces),
                                             (is_long, 2, long_first, long_end, pieces)):
            @pl.when(there)
            def _():
                @pl.loop(first, end)
                def _(k):
                    @pl.loop(0, some)
                    def _(p):
                        pass_on(box, k, p).wait_send()

    @pl.when((fwd & ~w_first) | (~fwd & ~e_first))
    def _():
        remote(eo_ref, eo_ref, send_sem.at[5], out_sem.at[0], other).wait_recv()


def flush(east, west, east_out, west_out, sem):
    copies = [pltpu.make_async_copy(a, b, sem.at[i])
              for i, (a, b) in enumerate(((east, east_out), (west, west_out)))]
    for copy in copies:
        copy.start()
    for copy in copies:
        copy.wait()


def local(rows, cols, operator, east_sources, west_sources):
    matrix = operator[0, 0]
    batch, width = east_sources.shape[2:]
    blocks, block_rows = BLOCKS, batch // BLOCKS
    cut = (blocks, block_rows, width)
    full = 2 * width
    piece = full // PIECES
    cells = (blocks, PIECES, block_rows, piece)
    trace = pltpu.VMEM(cells, jnp.bfloat16)
    slots = max(end - first for first, end, *_ in (*NEAR_LEAD, *NEAR_REST, LONG_LEAD, LONG_REST))
    dma = pltpu.SemaphoreType.DMA
    hbm = functools.partial(pltpu.with_memory_space_constraint, memory_space=pltpu.HBM)
    east, west = pl.pallas_call(
        functools.partial(sweeps, rows, cols),
        out_shape=[jax.ShapeDtypeStruct(cut, jnp.bfloat16)] * 2,
        in_specs=[pl.BlockSpec(memory_space=pltpu.HBM)] * 3,
        out_specs=[pl.BlockSpec(memory_space=pl.ANY)] * 2,
        scratch_shapes=[
            pltpu.VMEM((2, full // CHUNK, CHUNK, full), jnp.bfloat16),
            pltpu.VMEM((PIECES, blocks, block_rows, piece), jnp.bfloat16),
            trace,
            pltpu.VMEM((blocks + slots, *cells[1:]), jnp.bfloat16),
            trace,
            pltpu.VMEM((block_rows, full), jnp.float32),
            pltpu.VMEM((block_rows, piece), jnp.bfloat16),
            dma((full // CHUNK,)), dma((PIECES,)),
            dma((blocks, PIECES)), dma((blocks + slots, PIECES)),
            dma((1,)), dma((6,)), dma((2,)),
        ],
        compiler_params=pltpu.CompilerParams(
            collective_id=0, has_side_effects=True,
            vmem_limit_bytes=32 * 2**20),
        name="sweeps",
    )(hbm(matrix), hbm(east_sources.reshape(cut)), hbm(west_sources.reshape(cut)))
    anywhere = pl.BlockSpec(memory_space=pl.ANY)
    east, west = pl.pallas_call(
        flush,
        out_shape=[jax.ShapeDtypeStruct(cut, jnp.bfloat16)] * 2,
        in_specs=[anywhere] * 2,
        out_specs=[anywhere] * 2,
        scratch_shapes=[dma((2,))],
        compiler_params=pltpu.CompilerParams(vmem_limit_bytes=2**20),
        name="flush",
    )(east, west)
    return east.reshape(1, 1, batch, width), west.reshape(1, 1, batch, width)


def solution(mesh):
    in_specs = (
        P("crow", "ccol", "half", None),
        P("crow", "ccol", None, "half"),
        P("crow", "ccol", None, "half"),
    )
    out_specs = (P("crow", "ccol", None, "half"), P("crow", "ccol", None, "half"))
    body = functools.partial(local, mesh.shape["crow"], mesh.shape["ccol"])
    return jax.shard_map(body, mesh=mesh, in_specs=in_specs, out_specs=out_specs, check_vma=False)
```

```python
import functools

import jax
import jax.numpy as jnp
from jax import lax
from jax.experimental import pallas as pl
from jax.experimental.pallas import tpu as pltpu
from jax.sharding import PartitionSpec as P

BLOCKS = 12
PIECES = 4
CHUNK = 256
TILE = 256
NEAR_LEAD, NEAR_REST = ((12, 12, 4), (12, 12, 4), (12, 12, 4)), ((8, 12, 4), (12, 12, 4), (12, 12, 4))
LONG_LEAD, LONG_REST = (0, 9), (1, 6)
NEAR_OFF, BACK_OFF, AHEAD_OFF = 4, 8, -7
MESH = pl.DeviceIdType.MESH


def sweeps(rows, cols, op_ref, es_ref, ws_ref, eo_ref, wo_ref,
           mats, src, from_row, inbox, out, acc, zeros,
           op_sem, src_sem, row_sem, col_sem, out_sem, send_sem, keep_sem):
    row, col, half = lax.axis_index("crow"), lax.axis_index("ccol"), lax.axis_index("half")
    blocks, block_rows, width = es_ref.shape
    pieces, piece = from_row.shape[1], from_row.shape[3]
    mine = pieces // 2
    chunks, chunk, full = mats.shape[1:]
    own_chunks = chunks // 2
    per_piece = piece // chunk

    fwd = half == 0
    step = 1 - 2 * half
    last = cols - 1
    e_level = row + col
    w_level = rows - 1 - row + last - col
    level = jnp.where(fwd, e_level, w_level)
    e_first, w_first = e_level == 0, w_level == 0
    has_n, has_s, has_w, has_e = row > 0, row < rows - 1, col > 0, col < last
    up_row, dn_row = (fwd & has_n) | (~fwd & has_s), (fwd & has_s) | (~fwd & has_n)
    up_col, dn_col = (fwd & has_w) | (~fwd & has_e), (fwd & has_e) | (~fwd & has_w)
    next_row, next_col = {"crow": row + step}, {"ccol": col + step}
    other = {"half": 1 - half}

    place = jnp.where(fwd, col, last - col)
    lead = jnp.where(fwd, row == 0, row == rows - 1)
    turns = (cols - 1) // 2
    detour = turns > 0
    middle = 2 * (turns // 2) + 1
    odd = place % 2 == 1
    def pick(cases, default):
        for cond, value in cases:
            default = jnp.where(cond, value, default)
        return default

    def at(where_to):
        return {"ccol": jnp.where(fwd, where_to, last - where_to)}

    def near_of(turn):
        kind = pick(((turn < turns // 2, 0), (turn == turns // 2, 1)), 2)
        values = [pick([(lead & (kind == i), NEAR_LEAD[i][v]) for i in range(3)]
                       + [(~lead & (kind == i), NEAR_REST[i][v]) for i in range(3)], 0) for v in range(3)]
        return jnp.minimum(values[0], blocks), jnp.minimum(values[1], blocks), values[2]

    def long_of():
        first, end = (pick(((lead, LONG_LEAD[v]),), LONG_REST[v]) for v in range(2))
        return jnp.minimum(first, blocks), jnp.minimum(end, blocks)

    can_near = odd & (place < last)
    can_long = (place == middle) & (lead | (middle + 3 <= last))
    near_first, near_end, near_pieces = near_of(place // 2)
    long_first, long_end = long_of()
    long_base = jnp.where(lead, 0, blocks - long_first)
    long_place = jnp.where(lead, 0, middle + 3)
    is_near = ~odd & (place + 2 <= last)
    is_long = (place == long_place) & (middle + 1 <= last)
    to_near = ~odd & (place >= 2)
    to_long = (place == middle + 1) & (long_place <= last)

    def local(a, b, sem):
        return pltpu.make_async_copy(a, b, sem)

    def remote(a, b, send, recv, who):
        return pltpu.make_async_remote_copy(
            src_ref=a, dst_ref=b, send_sem=send, recv_sem=recv, device_id=who, device_id_type=MESH)

    zeros[...] = jnp.zeros_like(zeros)
    barrier = pltpu.get_barrier_semaphore()

    def greet(who):
        pl.semaphore_signal(barrier, inc=1, device_id=who, device_id_type=MESH)

    greet(other)
    for there, who in ((has_n, {"crow": row - 1}), (has_s, {"crow": row + 1}),
                       (has_w, {"ccol": col - 1}), (has_e, {"ccol": col + 1})):
        @pl.when(there)
        def _():
            for h in range(2):
                greet({**who, "half": h})
    count = 1 + 2 * (has_n.astype(jnp.int32) + has_s.astype(jnp.int32)
                     + has_w.astype(jnp.int32) + has_e.astype(jnp.int32))
    if detour:
        for there, whos in ((can_near, (place - 1,)), (is_near, (place + 1, place + 2)), (to_near, (place - 2,)),
                            (can_long, (long_place,)), (is_long, (middle, middle + 1)), (to_long, (long_place,))):
            @pl.when(there)
            def _():
                for who in whos:
                    greet(at(who))
            count += len(whos) * there.astype(jnp.int32)

    def op_own(c):
        return local(op_ref.at[pl.ds(c * chunk, chunk)], mats.at[0, half * own_chunks + c],
                     op_sem.at[half * own_chunks + c])

    def op_give(c):
        return remote(op_ref.at[pl.ds(c * chunk, chunk)], mats.at[0, half * own_chunks + c],
                      send_sem.at[0], op_sem.at[half * own_chunks + c], other)

    def op_wait(c):
        local(op_ref.at[pl.ds(0, chunk)], mats.at[0, c], op_sem.at[c]).wait()

    def src_own(ref, q):
        p = half * mine + q
        return local(ref.at[:, :, q * piece:(q + 1) * piece], src.at[p], src_sem.at[p])

    def src_give(ref, q):
        p = half * mine + q
        return remote(ref.at[:, :, q * piece:(q + 1) * piece], src.at[p], send_sem.at[1], src_sem.at[p], other)

    def first_to(ref, k, q, buffer, sem, send, who):
        p = half * mine + q
        return remote(ref.at[k, :, q * piece:(q + 1) * piece], buffer.at[k, p], send_sem.at[send], sem.at[k, p], who)

    def firsts(ref, k, shift, h):
        return [copy for q in range(mine) for copy in (
            first_to(ref, k, q, inbox, col_sem, 2, {"ccol": col + shift, "half": h}),
            first_to(ref, k, q, from_row, row_sem, 3, {"crow": row + shift, "half": h}))]

    @pl.when(~(e_first | w_first))
    def _():
        for c in range(own_chunks):
            op_own(c).start()
    pl.semaphore_wait(barrier, count)

    for there, ref, trace, shift, h in ((e_first, es_ref, eo_ref, 1, 0), (w_first, ws_ref, wo_ref, -1, 1)):
        @pl.when(there)
        def _():
            @pl.loop(0, blocks)
            def _(k):
                for copy in firsts(ref, k, shift, h):
                    copy.start()
            local(ref, trace, keep_sem.at[h]).start()

    for c in range(own_chunks):
        op_give(c).start()

    @pl.when(e_first | w_first)
    def _():
        for c in range(own_chunks):
            op_own(c).start()

    @pl.when(fwd)
    def _():
        for q in range(mine):
            src_own(es_ref, q).start()
            src_give(ws_ref, q).start()

    @pl.when(~fwd)
    def _():
        for q in range(mine):
            src_own(ws_ref, q).start()
            src_give(es_ref, q).start()

    share = pl.cdiv(blocks - 1, own_chunks)

    @pl.loop(0, chunks)
    def _(c):
        for there, buffer, sem in ((up_row, from_row, row_sem), (up_col, inbox, col_sem)):
            @pl.when((level > 0) & ~there)
            def _():
                begin = jnp.where(c < own_chunks, jnp.minimum(c, 1), 1 + share * (c - own_chunks))
                end = jnp.where(c < own_chunks, 1, begin + share)

                @pl.loop(jnp.minimum(begin, blocks), jnp.minimum(end, blocks))
                def _(k):
                    for p in range(pieces):
                        local(zeros, buffer.at[k, p], sem.at[k, p]).start()
        here = (c + half * own_chunks) % chunks
        op_wait(here)

        @pl.when(fwd & (level > 0))
        def _():
            at = pl.multiple_of(c * chunk, chunk)
            for n in range(chunks):
                mats[1, n, :, pl.ds(at, chunk)] = mats[0, c, :, n * chunk:(n + 1) * chunk].T
    for p in range(pieces):
        local(es_ref.at[:, :, :piece], src.at[p], src_sem.at[p]).wait()

    use = 1 - half

    def to_row(k, p):
        return remote(out.at[k, p], from_row.at[k, p], send_sem.at[3], row_sem.at[k, p], next_row)

    def to_col(k, p):
        by_near = can_near & (k >= near_first) & (k < near_end) & (p < near_pieces)
        by_long = can_long & (k >= long_first) & (k < long_end)
        slot = k + pick(((by_long, long_base), (by_near, blocks - near_first)), 0)
        who = at(pick(((by_long, long_place), (by_near, place - 1)), place + 1))
        return remote(out.at[k, p], inbox.at[slot, p], send_sem.at[2], col_sem.at[slot, p], who)

    def col_in(k, p):
        return local(zeros, inbox.at[k, p], col_sem.at[k, p])

    def row_in(k, p):
        return local(zeros, from_row.at[k, p], row_sem.at[k, p])

    def slot_of(box, k):
        return k + (blocks - hop_first if box == 1 else long_base)

    def via_in(box, k, p):
        return local(zeros, inbox.at[slot_of(box, k), p], col_sem.at[slot_of(box, k), p])

    def pass_on(box, k, p):
        return remote(inbox.at[slot_of(box, k), p], inbox.at[k, p], send_sem.at[4], col_sem.at[k, p],
                      at(place + 2 if box == 1 else middle + 1))

    def keep(trace, k, p):
        return local(out.at[k, p], trace.at[k, :, (p % mine) * piece:(p % mine + 1) * piece], keep_sem.at[half])

    def give(trace, k, p):
        return remote(out.at[k, p], trace.at[k, :, (p % mine) * piece:(p % mine + 1) * piece],
                      send_sem.at[5], out_sem.at[0], other)

    def send(k, some):
        @pl.when(dn_col)
        def _():
            for p in some:
                to_col(k, p).start()

        @pl.when(dn_row)
        def _():
            for p in some:
                to_row(k, p).start()

    def own(s, p):
        row_in(s, p).wait()
        col_in(s, p).wait()
        x = (from_row[s, p].astype(jnp.float32) + inbox[s, p].astype(jnp.float32)).astype(jnp.bfloat16)
        for n in range(0, full, TILE):
            weights = mats[use, p * per_piece:(p + 1) * per_piece, :, n:n + TILE].reshape(piece, TILE)
            part = jnp.dot(x, weights, preferred_element_type=jnp.float32)
            o, at = n // piece, n % piece
            if p == 0:
                acc[:, n:n + TILE] = part + src[o, s, :, at:at + TILE].astype(jnp.float32)
            elif p < pieces - 1:
                acc[:, n:n + TILE] += part
            else:
                out[s, o, :, at:at + TILE] = (acc[:, n:n + TILE] + part).astype(jnp.bfloat16)
                if n + TILE == piece:
                    send(s, (0,))
                if n + TILE == full:
                    send(s, range(1, pieces))

    def store(s):
        @pl.when(fwd)
        def _():
            for p in range(pieces):
                (keep if p < mine else give)(eo_ref, s, p).start()

        @pl.when(~fwd)
        def _():
            for p in range(pieces):
                (give if p < mine else keep)(wo_ref, s, p).start()

    hop_first, hop_end, hop_pieces = near_of(place // 2)
    long_off = jnp.where(lead, BACK_OFF, AHEAD_OFF)
    is_via = is_near & (hop_end > hop_first) | is_long & (long_end > long_first)

    def relay(t):
        @pl.when(is_via)
        def _():
            k = t - NEAR_OFF

            @pl.when(is_near & (k >= hop_first) & (k < hop_end))
            def _():
                @pl.loop(0, hop_pieces)
                def _(p):
                    via_in(1, k, p).wait()
                    pass_on(1, k, p).start()
            m = t - long_off

            @pl.when(is_long & (m >= long_first) & (m < long_end))
            def _():
                for p in range(pieces):
                    via_in(2, m, p).wait()
                    pass_on(2, m, p).start()

    if detour:
        @pl.loop(min(AHEAD_OFF, 0), 0)
        def _(t):
            relay(t)

    @pl.when(level > 0)
    def _():
        @pl.loop(0, blocks)
        def _(s):
            for p in range(pieces):
                own(s, p)
            store(s)
            if detour:
                relay(s)

    if detour:
        @pl.loop(jnp.where(level > 0, blocks, 0), blocks + max(NEAR_OFF, BACK_OFF))
        def _(t):
            relay(t)

    for c in range(own_chunks):
        op_give(c).wait_send()
    for q in range(mine):
        src_give(es_ref, q).wait_send()
    for there, ref, trace, shift, h in ((e_first, es_ref, eo_ref, 1, 0), (w_first, ws_ref, wo_ref, -1, 1)):
        @pl.when(there)
        def _():
            @pl.loop(0, blocks)
            def _(k):
                for copy in firsts(ref, k, shift, h):
                    copy.wait_send()
            local(ref, trace, keep_sem.at[h]).wait()

    @pl.when(level > 0)
    def _():
        @pl.when(dn_row)
        def _():
            remote(out, from_row, send_sem.at[3], row_sem.at[0, 0], next_row).wait_send()

        @pl.when(dn_col)
        def _():
            remote(out, from_row, send_sem.at[2], row_sem.at[0, 0], next_col).wait_send()
        local(eo_ref, eo_ref, keep_sem.at[half]).wait()
        remote(eo_ref, eo_ref, send_sem.at[5], out_sem.at[0], other).wait_send()
    if detour:
        for there, box, first, end, some in ((is_near, 1, hop_first, hop_end, hop_pieces),
                                             (is_long, 2, long_first, long_end, pieces)):
            @pl.when(there)
            def _():
                @pl.loop(first, end)
                def _(k):
                    @pl.loop(0, some)
                    def _(p):
                        pass_on(box, k, p).wait_send()

    @pl.when((fwd & ~w_first) | (~fwd & ~e_first))
    def _():
        remote(eo_ref, eo_ref, send_sem.at[5], out_sem.at[0], other).wait_recv()


def flush(east, west, east_out, west_out, sem):
    copies = [pltpu.make_async_copy(a, b, sem.at[i])
              for i, (a, b) in enumerate(((east, east_out), (west, west_out)))]
    for copy in copies:
        copy.start()
    for copy in copies:
        copy.wait()


def local(rows, cols, operator, east_sources, west_sources):
    matrix = operator[0, 0]
    batch, width = east_sources.shape[2:]
    blocks, block_rows = BLOCKS, batch // BLOCKS
    cut = (blocks, block_rows, width)
    full = 2 * width
    piece = full // PIECES
    cells = (blocks, PIECES, block_rows, piece)
    trace = pltpu.VMEM(cells, jnp.bfloat16)
    slots = max(end - first for first, end, *_ in (*NEAR_LEAD, *NEAR_REST, LONG_REST))
    dma = pltpu.SemaphoreType.DMA
    hbm = functools.partial(pltpu.with_memory_space_constraint, memory_space=pltpu.HBM)
    east, west = pl.pallas_call(
        functools.partial(sweeps, rows, cols),
        out_shape=[jax.ShapeDtypeStruct(cut, jnp.bfloat16)] * 2,
        in_specs=[pl.BlockSpec(memory_space=pltpu.HBM)] * 3,
        out_specs=[pl.BlockSpec(memory_space=pl.ANY)] * 2,
        scratch_shapes=[
            pltpu.VMEM((2, full // CHUNK, CHUNK, full), jnp.bfloat16),
            pltpu.VMEM((PIECES, blocks, block_rows, piece), jnp.bfloat16),
            trace,
            pltpu.VMEM((blocks + slots, *cells[1:]), jnp.bfloat16),
            trace,
            pltpu.VMEM((block_rows, full), jnp.float32),
            pltpu.VMEM((block_rows, piece), jnp.bfloat16),
            dma((full // CHUNK,)), dma((PIECES,)),
            dma((blocks, PIECES)), dma((blocks + slots, PIECES)),
            dma((1,)), dma((6,)), dma((2,)),
        ],
        compiler_params=pltpu.CompilerParams(
            collective_id=0, has_side_effects=True,
            vmem_limit_bytes=32 * 2**20),
        name="sweeps",
    )(hbm(matrix), hbm(east_sources.reshape(cut)), hbm(west_sources.reshape(cut)))
    anywhere = pl.BlockSpec(memory_space=pl.ANY)
    east, west = pl.pallas_call(
        flush,
        out_shape=[jax.ShapeDtypeStruct(cut, jnp.bfloat16)] * 2,
        in_specs=[anywhere] * 2,
        out_specs=[anywhere] * 2,
        scratch_shapes=[dma((2,))],
        compiler_params=pltpu.CompilerParams(vmem_limit_bytes=2**20),
        name="flush",
    )(east, west)
    return east.reshape(1, 1, batch, width), west.reshape(1, 1, batch, width)


def solution(mesh):
    in_specs = (
        P("crow", "ccol", "half", None),
        P("crow", "ccol", None, "half"),
        P("crow", "ccol", None, "half"),
    )
    out_specs = (P("crow", "ccol", None, "half"), P("crow", "ccol", None, "half"))
    body = functools.partial(local, mesh.shape["crow"], mesh.shape["ccol"])
    return jax.shard_map(body, mesh=mesh, in_specs=in_specs, out_specs=out_specs, check_vma=False)
```

```python
import functools

import jax
import jax.numpy as jnp
from jax import lax
from jax.experimental import pallas as pl
from jax.experimental.pallas import tpu as pltpu
from jax.sharding import PartitionSpec as P

BLOCKS = 12
PIECES = 4
CHUNK = 256
TILE = 256
NEAR_LEAD, NEAR_REST = ((12, 12, 4), (12, 12, 4), (12, 12, 4)), ((8, 12, 4), (12, 12, 4), (12, 12, 4))
LONG_LEAD, LONG_REST = (0, 9), (1, 6)
NEAR_OFF, BACK_OFF, AHEAD_OFF = 4, 8, -7
MESH = pl.DeviceIdType.MESH


def sweeps(rows, cols, op_ref, es_ref, ws_ref, eo_ref, wo_ref,
           mats, src, from_row, inbox, out, acc, zeros,
           op_sem, src_sem, row_sem, col_sem, out_sem, send_sem, keep_sem):
    row, col, half = lax.axis_index("crow"), lax.axis_index("ccol"), lax.axis_index("half")
    blocks, block_rows, width = es_ref.shape
    pieces, piece = from_row.shape[1], from_row.shape[3]
    mine = pieces // 2
    chunks, chunk, full = mats.shape[1:]
    own_chunks = chunks // 2
    per_piece = piece // chunk

    fwd = half == 0
    step = 1 - 2 * half
    last = cols - 1
    e_level = row + col
    w_level = rows - 1 - row + last - col
    level = jnp.where(fwd, e_level, w_level)
    e_first, w_first = e_level == 0, w_level == 0
    has_n, has_s, has_w, has_e = row > 0, row < rows - 1, col > 0, col < last
    up_row, dn_row = (fwd & has_n) | (~fwd & has_s), (fwd & has_s) | (~fwd & has_n)
    up_col, dn_col = (fwd & has_w) | (~fwd & has_e), (fwd & has_e) | (~fwd & has_w)
    next_row, next_col = {"crow": row + step}, {"ccol": col + step}
    other = {"half": 1 - half}

    place = jnp.where(fwd, col, last - col)
    lead = jnp.where(fwd, row == 0, row == rows - 1)
    turns = (cols - 1) // 2
    detour = turns > 0
    middle = 2 * (turns // 2) + 1
    odd = place % 2 == 1
    def pick(cases, default):
        for cond, value in cases:
            default = jnp.where(cond, value, default)
        return default

    def at(where_to):
        return {"ccol": jnp.where(fwd, where_to, last - where_to)}

    def near_of(turn):
        kind = pick(((turn < turns // 2, 0), (turn == turns // 2, 1)), 2)
        values = [pick([(lead & (kind == i), NEAR_LEAD[i][v]) for i in range(3)]
                       + [(~lead & (kind == i), NEAR_REST[i][v]) for i in range(3)], 0) for v in range(3)]
        return jnp.minimum(values[0], blocks), jnp.minimum(values[1], blocks), values[2]

    def long_of():
        first, end = (pick(((lead, LONG_LEAD[v]),), LONG_REST[v]) for v in range(2))
        return jnp.minimum(first, blocks), jnp.minimum(end, blocks)

    can_near = odd & (place < last)
    can_long = (place == middle) & (lead | (middle + 3 <= last))
    near_first, near_end, near_pieces = near_of(place // 2)
    long_first, long_end = long_of()
    long_base = jnp.where(lead, 0, blocks - long_first)
    long_place = jnp.where(lead, 0, middle + 3)
    is_near = ~odd & (place + 2 <= last)
    is_long = (place == long_place) & (middle + 1 <= last)
    to_near = ~odd & (place >= 2)
    to_long = (place == middle + 1) & (long_place <= last)

    def local(a, b, sem):
        return pltpu.make_async_copy(a, b, sem)

    def remote(a, b, send, recv, who):
        return pltpu.make_async_remote_copy(
            src_ref=a, dst_ref=b, send_sem=send, recv_sem=recv, device_id=who, device_id_type=MESH)

    zeros[...] = jnp.zeros_like(zeros)
    barrier = pltpu.get_barrier_semaphore()

    def greet(who):
        pl.semaphore_signal(barrier, inc=1, device_id=who, device_id_type=MESH)

    greet(other)
    for there, who in ((has_n, {"crow": row - 1}), (has_s, {"crow": row + 1}),
                       (has_w, {"ccol": col - 1}), (has_e, {"ccol": col + 1})):
        @pl.when(there)
        def _():
            for h in range(2):
                greet({**who, "half": h})
    count = 1 + 2 * (has_n.astype(jnp.int32) + has_s.astype(jnp.int32)
                     + has_w.astype(jnp.int32) + has_e.astype(jnp.int32))
    if detour:
        for there, whos in ((can_near, (place - 1,)), (is_near, (place + 1, place + 2)), (to_near, (place - 2,)),
                            (can_long, (long_place,)), (is_long, (middle, middle + 1)), (to_long, (long_place,))):
            @pl.when(there)
            def _():
                for who in whos:
                    greet(at(who))
            count += len(whos) * there.astype(jnp.int32)

    def op_own(c):
        return local(op_ref.at[pl.ds(c * chunk, chunk)], mats.at[0, half * own_chunks + c],
                     op_sem.at[half * own_chunks + c])

    def op_give(c):
        return remote(op_ref.at[pl.ds(c * chunk, chunk)], mats.at[0, half * own_chunks + c],
                      send_sem.at[0], op_sem.at[half * own_chunks + c], other)

    def op_wait(c):
        local(op_ref.at[pl.ds(0, chunk)], mats.at[0, c], op_sem.at[c]).wait()

    def part_of(part):
        return pl.ds(part, 1 if part == 0 else blocks - 1)

    def src_own(ref, q, part):
        p = half * mine + q
        return local(ref.at[part_of(part), :, q * piece:(q + 1) * piece], src.at[p, part_of(part)], src_sem.at[part, p])

    def src_give(ref, q, part):
        p = half * mine + q
        return remote(ref.at[part_of(part), :, q * piece:(q + 1) * piece], src.at[p, part_of(part)],
                      send_sem.at[1], src_sem.at[part, p], other)

    def src_wait(part):
        for p in range(pieces):
            local(es_ref.at[part_of(part), :, :piece], src.at[p, part_of(part)], src_sem.at[part, p]).wait()

    def src_start(part):
        for there, stay, go in ((fwd, es_ref, ws_ref), (~fwd, ws_ref, es_ref)):
            @pl.when(there)
            def _():
                for q in range(mine):
                    src_own(stay, q, part).start()
                    src_give(go, q, part).start()

    def first_to(ref, k, q, buffer, sem, send, who):
        p = half * mine + q
        return remote(ref.at[k, :, q * piece:(q + 1) * piece], buffer.at[k, p], send_sem.at[send], sem.at[k, p], who)

    def firsts(ref, k, shift, h):
        return [copy for q in range(mine) for copy in (
            first_to(ref, k, q, inbox, col_sem, 2, {"ccol": col + shift, "half": h}),
            first_to(ref, k, q, from_row, row_sem, 3, {"crow": row + shift, "half": h}))]

    @pl.when(~(e_first | w_first))
    def _():
        for c in range(own_chunks):
            op_own(c).start()
    pl.semaphore_wait(barrier, count)

    for there, ref, trace, shift, h in ((e_first, es_ref, eo_ref, 1, 0), (w_first, ws_ref, wo_ref, -1, 1)):
        @pl.when(there)
        def _():
            @pl.loop(0, blocks)
            def _(k):
                for copy in firsts(ref, k, shift, h):
                    copy.start()
            local(ref, trace, keep_sem.at[h]).start()

    src_start(0)
    for c in range(own_chunks):
        op_give(c).start()

    @pl.when(e_first | w_first)
    def _():
        for c in range(own_chunks):
            op_own(c).start()

    src_start(1)
    share = pl.cdiv(blocks - 1, own_chunks)

    @pl.loop(0, chunks)
    def _(c):
        for there, buffer, sem in ((up_row, from_row, row_sem), (up_col, inbox, col_sem)):
            @pl.when((level > 0) & ~there)
            def _():
                begin = jnp.where(c < own_chunks, jnp.minimum(c, 1), 1 + share * (c - own_chunks))
                end = jnp.where(c < own_chunks, 1, begin + share)

                @pl.loop(jnp.minimum(begin, blocks), jnp.minimum(end, blocks))
                def _(k):
                    for p in range(pieces):
                        local(zeros, buffer.at[k, p], sem.at[k, p]).start()
        here = (c + half * own_chunks) % chunks
        op_wait(here)

        @pl.when(fwd & (level > 0))
        def _():
            at = pl.multiple_of(c * chunk, chunk)
            for n in range(chunks):
                mats[1, n, :, pl.ds(at, chunk)] = mats[0, c, :, n * chunk:(n + 1) * chunk].T
    src_wait(0)

    @pl.when(level == 0)
    def _():
        src_wait(1)

    use = 1 - half

    def to_row(k, p):
        return remote(out.at[k, p], from_row.at[k, p], send_sem.at[3], row_sem.at[k, p], next_row)

    def to_col(k, p):
        by_near = can_near & (k >= near_first) & (k < near_end) & (p < near_pieces)
        by_long = can_long & (k >= long_first) & (k < long_end)
        slot = k + pick(((by_long, long_base), (by_near, blocks - near_first)), 0)
        who = at(pick(((by_long, long_place), (by_near, place - 1)), place + 1))
        return remote(out.at[k, p], inbox.at[slot, p], send_sem.at[2], col_sem.at[slot, p], who)

    def col_in(k, p):
        return local(zeros, inbox.at[k, p], col_sem.at[k, p])

    def row_in(k, p):
        return local(zeros, from_row.at[k, p], row_sem.at[k, p])

    def slot_of(box, k):
        return k + (blocks - hop_first if box == 1 else long_base)

    def via_in(box, k, p):
        return local(zeros, inbox.at[slot_of(box, k), p], col_sem.at[slot_of(box, k), p])

    def pass_on(box, k, p):
        return remote(inbox.at[slot_of(box, k), p], inbox.at[k, p], send_sem.at[4], col_sem.at[k, p],
                      at(place + 2 if box == 1 else middle + 1))

    def keep(trace, k, p):
        return local(out.at[k, p], trace.at[k, :, (p % mine) * piece:(p % mine + 1) * piece], keep_sem.at[half])

    def give(trace, k, p):
        return remote(out.at[k, p], trace.at[k, :, (p % mine) * piece:(p % mine + 1) * piece],
                      send_sem.at[5], out_sem.at[0], other)

    def send(k, some):
        @pl.when(dn_col)
        def _():
            for p in some:
                to_col(k, p).start()

        @pl.when(dn_row)
        def _():
            for p in some:
                to_row(k, p).start()

    def own(s, p):
        row_in(s, p).wait()
        col_in(s, p).wait()
        x = (from_row[s, p].astype(jnp.float32) + inbox[s, p].astype(jnp.float32)).astype(jnp.bfloat16)
        for n in range(0, full, TILE):
            weights = mats[use, p * per_piece:(p + 1) * per_piece, :, n:n + TILE].reshape(piece, TILE)
            part = jnp.dot(x, weights, preferred_element_type=jnp.float32)
            o, at = n // piece, n % piece
            if p == 0:
                acc[:, n:n + TILE] = part + src[o, s, :, at:at + TILE].astype(jnp.float32)
            elif p < pieces - 1:
                acc[:, n:n + TILE] += part
            else:
                out[s, o, :, at:at + TILE] = (acc[:, n:n + TILE] + part).astype(jnp.bfloat16)
                if n + TILE == piece:
                    send(s, (0,))
                if n + TILE == full:
                    send(s, range(1, pieces))

    def store(s):
        @pl.when(fwd)
        def _():
            @pl.when(s == 0)
            def _():
                src_wait(1)
            for p in range(pieces):
                (keep if p < mine else give)(eo_ref, s, p).start()

        @pl.when(~fwd)
        def _():
            @pl.when(s == 0)
            def _():
                src_wait(1)
            for p in range(pieces):
                (give if p < mine else keep)(wo_ref, s, p).start()

    hop_first, hop_end, hop_pieces = near_of(place // 2)
    long_off = jnp.where(lead, BACK_OFF, AHEAD_OFF)
    is_via = is_near & (hop_end > hop_first) | is_long & (long_end > long_first)

    def relay(t):
        @pl.when(is_via)
        def _():
            k = t - NEAR_OFF

            @pl.when(is_near & (k >= hop_first) & (k < hop_end))
            def _():
                @pl.loop(0, hop_pieces)
                def _(p):
                    via_in(1, k, p).wait()
                    pass_on(1, k, p).start()
            m = t - long_off

            @pl.when(is_long & (m >= long_first) & (m < long_end))
            def _():
                for p in range(pieces):
                    via_in(2, m, p).wait()
                    pass_on(2, m, p).start()

    if detour:
        @pl.loop(min(AHEAD_OFF, 0), 0)
        def _(t):
            relay(t)

    @pl.when(level > 0)
    def _():
        @pl.loop(0, blocks)
        def _(s):
            for p in range(pieces):
                own(s, p)
            store(s)
            if detour:
                relay(s)

    if detour:
        @pl.loop(jnp.where(level > 0, blocks, 0), blocks + max(NEAR_OFF, BACK_OFF))
        def _(t):
            relay(t)

    for c in range(own_chunks):
        op_give(c).wait_send()
    for q in range(mine):
        for part in range(2):
            src_give(es_ref, q, part).wait_send()
    for there, ref, trace, shift, h in ((e_first, es_ref, eo_ref, 1, 0), (w_first, ws_ref, wo_ref, -1, 1)):
        @pl.when(there)
        def _():
            @pl.loop(0, blocks)
            def _(k):
                for copy in firsts(ref, k, shift, h):
                    copy.wait_send()
            local(ref, trace, keep_sem.at[h]).wait()

    @pl.when(level > 0)
    def _():
        @pl.when(dn_row)
        def _():
            remote(out, from_row, send_sem.at[3], row_sem.at[0, 0], next_row).wait_send()

        @pl.when(dn_col)
        def _():
            remote(out, from_row, send_sem.at[2], row_sem.at[0, 0], next_col).wait_send()
        local(eo_ref, eo_ref, keep_sem.at[half]).wait()
        remote(eo_ref, eo_ref, send_sem.at[5], out_sem.at[0], other).wait_send()
    if detour:
        for there, box, first, end, some in ((is_near, 1, hop_first, hop_end, hop_pieces),
                                             (is_long, 2, long_first, long_end, pieces)):
            @pl.when(there)
            def _():
                @pl.loop(first, end)
                def _(k):
                    @pl.loop(0, some)
                    def _(p):
                        pass_on(box, k, p).wait_send()

    @pl.when((fwd & ~w_first) | (~fwd & ~e_first))
    def _():
        remote(eo_ref, eo_ref, send_sem.at[5], out_sem.at[0], other).wait_recv()


def flush(east, west, east_out, west_out, sem):
    copies = [pltpu.make_async_copy(a, b, sem.at[i])
              for i, (a, b) in enumerate(((east, east_out), (west, west_out)))]
    for copy in copies:
        copy.start()
    for copy in copies:
        copy.wait()


def local(rows, cols, operator, east_sources, west_sources):
    matrix = operator[0, 0]
    batch, width = east_sources.shape[2:]
    blocks, block_rows = BLOCKS, batch // BLOCKS
    cut = (blocks, block_rows, width)
    full = 2 * width
    piece = full // PIECES
    cells = (blocks, PIECES, block_rows, piece)
    trace = pltpu.VMEM(cells, jnp.bfloat16)
    slots = max(end - first for first, end, *_ in (*NEAR_LEAD, *NEAR_REST, LONG_REST))
    dma = pltpu.SemaphoreType.DMA
    hbm = functools.partial(pltpu.with_memory_space_constraint, memory_space=pltpu.HBM)
    east, west = pl.pallas_call(
        functools.partial(sweeps, rows, cols),
        out_shape=[jax.ShapeDtypeStruct(cut, jnp.bfloat16)] * 2,
        in_specs=[pl.BlockSpec(memory_space=pltpu.HBM)] * 3,
        out_specs=[pl.BlockSpec(memory_space=pl.ANY)] * 2,
        scratch_shapes=[
            pltpu.VMEM((2, full // CHUNK, CHUNK, full), jnp.bfloat16),
            pltpu.VMEM((PIECES, blocks, block_rows, piece), jnp.bfloat16),
            trace,
            pltpu.VMEM((blocks + slots, *cells[1:]), jnp.bfloat16),
            trace,
            pltpu.VMEM((block_rows, full), jnp.float32),
            pltpu.VMEM((block_rows, piece), jnp.bfloat16),
            dma((full // CHUNK,)), dma((2, PIECES)),
            dma((blocks, PIECES)), dma((blocks + slots, PIECES)),
            dma((1,)), dma((6,)), dma((2,)),
        ],
        compiler_params=pltpu.CompilerParams(
            collective_id=0, has_side_effects=True,
            vmem_limit_bytes=32 * 2**20),
        name="sweeps",
    )(hbm(matrix), hbm(east_sources.reshape(cut)), hbm(west_sources.reshape(cut)))
    anywhere = pl.BlockSpec(memory_space=pl.ANY)
    east, west = pl.pallas_call(
        flush,
        out_shape=[jax.ShapeDtypeStruct(cut, jnp.bfloat16)] * 2,
        in_specs=[anywhere] * 2,
        out_specs=[anywhere] * 2,
        scratch_shapes=[dma((2,))],
        compiler_params=pltpu.CompilerParams(vmem_limit_bytes=2**20),
        name="flush",
    )(east, west)
    return east.reshape(1, 1, batch, width), west.reshape(1, 1, batch, width)


def solution(mesh):
    in_specs = (
        P("crow", "ccol", "half", None),
        P("crow", "ccol", None, "half"),
        P("crow", "ccol", None, "half"),
    )
    out_specs = (P("crow", "ccol", None, "half"), P("crow", "ccol", None, "half"))
    body = functools.partial(local, mesh.shape["crow"], mesh.shape["ccol"])
    return jax.shard_map(body, mesh=mesh, in_specs=in_specs, out_specs=out_specs, check_vma=False)
```
